128 devices in a mesh: chan: 16 (over x_hi, z, core), tm: 8 (over x_lo, y).
Axes of the slice: x: 4 (x_hi: 2, x_lo: 2; x = x_hi * 2 + x_lo), y: 4, z: 4, core: 2. Of those that a mesh axis runs over, the one named last changes fastest.
Arguments:
- spectra: bfloat16 [1792, 32, 16, 2, 256], P('tm', None, 'chan'), may hold values from -6 to 6
- partner: int32 [3, 16], replicated, may hold values from 0 to 15, as said below
Outputs:
- stacks: float32 [3, 16, 16, 2, 256, 256], P(None, 'chan', 'tm')
The draws below stay inside these ranges and needn't reach their ends.
Inputs may be any that keep to these rules, and one draw needn't show every extreme that they name: `partner`: each of the 3 rows pairs the 16 blocks off: entry i is j exactly when entry j is i, and never i; no two rows pair the same two blocks.
All inputs are finite; a program needn't handle non-finite values.
Results may differ from the reference program's by a relative error of at most 0.0003.
Values may be sent and summed in bfloat16 or wider, within the bound.
No kernel may reach another device: no remote copies, remote signals or barrier semaphores. Data moves between devices by JAX's collectives and lax.ppermute only.
A program may use at most 128 MiB of HBM per device.

```python
import math
import jax
import jax.numpy as jnp
from jax import lax

CB = 256
BINS = 32
ROUNDS = 3
BLOCKS = 16
WINDOWS = 1792
HALF = 16


def draw_partner(key, part):
    first_key, second_key = jax.random.split(jax.random.fold_in(key, 17))
    order = jax.random.permutation(first_key, BLOCKS).astype(jnp.int32)
    places = jnp.zeros((BLOCKS,), jnp.int32).at[order].set(jnp.arange(BLOCKS, dtype=jnp.int32))
    circle = BLOCKS - 1
    offset = jax.random.randint(second_key, (), 0, circle).astype(jnp.int32)
    rows = []
    for step in range(ROUNDS):
        turn = (offset + step) % circle
        mate = (2 * turn - places) % circle
        mate = jnp.where(mate == places, circle, mate)
        mate = jnp.where(places == circle, turn, mate)
        rows.append(order[mate])
    return jnp.stack(rows).astype(jnp.int32)


def steps_of(rng, dims, cuts, smallest, largest):
    loudness = 1.0
    for axis_at, parts in cuts:
        heights = jax.random.uniform(jax.random.fold_in(jax.random.fold_in(rng, 6), axis_at), (parts,), jnp.float32, smallest / len(cuts), largest / len(cuts))
        loudness = loudness * jnp.repeat(jnp.exp(heights), dims[axis_at] // parts).reshape((-1,) + (1,) * (len(dims) - 1 - axis_at))
    return loudness


def bell_draw(stream_key, dims, spread, bound, shards=(), kind=jnp.bfloat16):
    factor_of = steps_of(stream_key, dims, shards, -0.22, 0.18) if shards else 1.0
    result = jax.random.normal(stream_key, dims, jnp.float32) * spread * factor_of
    return jnp.minimum(jnp.maximum(result, -bound), bound).astype(kind)


def setup_inputs(seed: int = 0) -> dict:
    keys = jax.random.split(jax.random.key(seed), 3)
    return {
        "spectra": bell_draw(keys[0], (WINDOWS, BINS, BLOCKS, 2, CB), 1.0, 6.0, ((0, 8), (2, 16))),
        "partner": draw_partner(jax.random.fold_in(keys[2], 71), 0),
    }


def block_stack(spectra, round_row, block):
    other_block = round_row[block]
    half = (block > other_block).astype(jnp.int32)
    zero = jnp.int32(0)
    start = (half * HALF).astype(jnp.int32)
    own_side = lax.dynamic_slice(spectra, (zero, start, block.astype(jnp.int32), zero, zero), (WINDOWS, HALF, 1, 2, CB))
    far_side = lax.dynamic_slice(spectra, (zero, start, other_block.astype(jnp.int32), zero, zero), (WINDOWS, HALF, 1, 2, CB))
    own_side = own_side.reshape(WINDOWS, HALF, 2 * CB).astype(jnp.float32)
    far_side = far_side.reshape(WINDOWS, HALF, 2 * CB).astype(jnp.float32)
    product = jnp.einsum('wfa,wfb->fab', own_side, far_side)
    real_part = product[:, :CB, :CB] + product[:, CB:, CB:]
    imag_part = product[:, CB:, :CB] - product[:, :CB, CB:]
    scale = 1.0 / math.sqrt(WINDOWS)
    return jnp.stack([real_part, imag_part], axis=1) * scale

def reference(spectra, partner):
    every_block = jnp.arange(BLOCKS, dtype=jnp.int32)
    results = []
    for round_index in range(ROUNDS):
        round_row = partner[round_index]
        results.append(lax.map(lambda block: block_stack(spectra, round_row, block), every_block))
    return jnp.stack(results)
```

```python
import math

import jax
import jax.numpy as jnp
from jax import lax
from jax.sharding import PartitionSpec as P


def per_device(spectra, partner):
    window_count, bins, _, _, width = spectra.shape
    blocks = lax.axis_size("chan")
    groups = lax.axis_size("tm")
    position = lax.axis_index("chan")
    rounds = partner.shape[0]
    half_bins = bins // 2
    mine_bins = half_bins // groups
    halves = (jnp.arange(blocks, dtype=jnp.int32)[None, :] > partner).astype(jnp.int32)
    arranged = spectra.reshape(window_count, 2, groups, mine_bins, 2 * width)
    arranged = arranged.transpose(2, 1, 3, 0, 4)
    gathered = lax.all_to_all(arranged, "tm", split_axis=0, concat_axis=0, tiled=True)
    share = window_count * groups // blocks
    shares = gathered.reshape(groups, 2, mine_bins, blocks // groups, share, 2 * width)
    shares = shares.transpose(0, 3, 1, 2, 4, 5).reshape(blocks, 2, mine_bins, share, 2 * width)
    holdings = lax.all_to_all(shares, "chan", split_axis=0, concat_axis=0, tiled=True)
    scale = 1.0 / math.sqrt(window_count * groups)
    results = []
    for r in range(rounds):
        outgoing = holdings[partner[r], halves[r]]
        incoming = lax.all_to_all(outgoing, "chan", split_axis=0, concat_axis=0, tiled=True)
        own = lax.dynamic_index_in_dim(shares, halves[r][position], 1, keepdims=False)
        product = jnp.einsum("jfwa,jfwb->fab", own, incoming, preferred_element_type=jnp.float32)
        real_part = product[:, :width, :width] + product[:, width:, width:]
        imag_part = product[:, width:, :width] - product[:, :width, width:]
        results.append(jnp.stack([real_part, imag_part], axis=1) * scale)
    return jnp.stack(results)[:, None]


def solution(mesh):
    placed = (P("tm", None, "chan", None, None), P())
    return jax.shard_map(
        per_device,
        mesh=mesh,
        in_specs=placed,
        out_specs=P(None, "chan", "tm", None, None, None),
        check_vma=False,
    )
```

```python
import functools
import math

import jax
import jax.numpy as jnp
from jax import lax
from jax.experimental import pallas as pl
from jax.experimental.pallas import tpu as pltpu
from jax.sharding import Mesh, PartitionSpec as P


ALL = ("xh", "z", "core", "xl", "y")
ZC = ("z", "core")
XY = ("xh", "xl", "y")
LANES = 128


def pack_kernel(groups, src, dst, buf, in_sem, out_sem):
    quarters, quarter, bins = buf.shape[:3]
    per = bins // 2 // groups

    def load(s):
        return pltpu.make_async_copy(src.at[pl.ds(s * quarter, quarter), :, 0], buf.at[s], in_sem.at[s])

    for s in range(quarters):
        load(s).start()
    for s in range(quarters):
        load(s).wait()
        for b in range(bins):
            h, rest = b // (bins // 2), b % (bins // 2)
            u, e = rest // per, rest % per
            for lh in range(buf.shape[-1] // LANES):
                pltpu.make_async_copy(
                    buf.at[s, :, b, :, pl.ds(lh * LANES, LANES)],
                    dst.at[s // 2, s % 2, e, lh, u, h],
                    out_sem.at[s],
                ).start()
    for s in range(quarters):
        pltpu.make_async_copy(src.at[pl.ds(s * quarter, quarter), :, 0], buf.at[s], out_sem.at[s]).wait()


def pack(spectra, groups):
    windows, bins, _, parts, width = spectra.shape
    quarter = windows // 4
    per, sides = bins // 2 // groups, width // LANES
    return pl.pallas_call(
        functools.partial(pack_kernel, groups),
        out_shape=jax.ShapeDtypeStruct((2, 2, per, sides, groups, 2, quarter, parts, LANES), spectra.dtype),
        in_specs=[pl.BlockSpec(memory_space=pl.ANY)],
        out_specs=pl.BlockSpec(memory_space=pl.ANY),
        scratch_shapes=[
            pltpu.VMEM((4, quarter, bins, parts, width), spectra.dtype),
            pltpu.SemaphoreType.DMA((4,)),
            pltpu.SemaphoreType.DMA((4,)),
        ],
        cost_estimate=pl.CostEstimate(flops=0, transcendentals=0, bytes_accessed=4 * spectra.size),
        name="pack",
    )(spectra)


def pick_kernel(blocks_ref, halves_ref, src, dst, buf, in_sem, out_sem):
    count = buf.shape[0]

    def load(i):
        return pltpu.make_async_copy(src.at[blocks_ref[i], :, halves_ref[i]], buf.at[i], in_sem.at[i])

    def store(i):
        return pltpu.make_async_copy(buf.at[i], dst.at[i], out_sem.at[i])

    for i in range(count):
        load(i).start()
    for i in range(count):
        load(i).wait()
        store(i).start()
    for i in range(count):
        store(i).wait()


def pick(holdings, chosen, halves):
    _, groups, _, rows, lanes = holdings.shape
    count = chosen.shape[0]
    shape = (count, groups, rows, lanes)
    return pl.pallas_call(
        pick_kernel,
        out_shape=jax.ShapeDtypeStruct(shape, holdings.dtype),
        grid_spec=pltpu.PrefetchScalarGridSpec(
            num_scalar_prefetch=2,
            grid=(),
            in_specs=[pl.BlockSpec(memory_space=pl.ANY)],
            out_specs=pl.BlockSpec(memory_space=pl.ANY),
            scratch_shapes=[
                pltpu.VMEM(shape, holdings.dtype),
                pltpu.SemaphoreType.DMA((count,)),
                pltpu.SemaphoreType.DMA((count,)),
            ],
        ),
        cost_estimate=pl.CostEstimate(flops=0, transcendentals=0, bytes_accessed=4 * math.prod(shape)),
        name="pick",
    )(chosen, halves, holdings)


def cross_kernel(where_ref, own_ref, other_ref, out_ref):
    groups, quarters, sides, rows, lanes = own_ref.shape
    depth = groups * rows
    odd = lax.broadcasted_iota(jnp.int32, (depth // 8, 8, lanes * sides), 1) % 2 == 1
    real = None
    for q in range(quarters):
        a = jnp.concatenate([own_ref[:, q, s].reshape(depth, lanes) for s in range(sides)], axis=1)
        b = jnp.concatenate([other_ref[q, s].reshape(depth, lanes) for s in range(sides)], axis=1)
        tall = b.astype(jnp.float32).reshape(depth // 8, 8, lanes * sides)
        turned = jnp.where(odd, pltpu.roll(tall, 1, 1), -pltpu.roll(tall, 7, 1))
        turned = turned.reshape(depth, lanes * sides).astype(b.dtype)
        dims = (((0,), (0,)), ((), ()))
        re = lax.dot_general(a, b, dims, preferred_element_type=jnp.float32)
        im = lax.dot_general(a, turned, dims, preferred_element_type=jnp.float32)
        real, imag = (re, im) if real is None else (real + re, imag + im)
    out_ref[0, 0] = real
    out_ref[0, 1] = imag


def cross(own, other, half, turn):
    groups, quarters, mine, sides, _, rows, lanes = own.shape
    width = sides * lanes
    read = groups * quarters * mine * sides * rows * lanes * 2
    return pl.pallas_call(
        cross_kernel,
        out_shape=jax.ShapeDtypeStruct((mine, 2, width, width), jnp.float32),
        grid_spec=pltpu.PrefetchScalarGridSpec(
            num_scalar_prefetch=1,
            grid=(mine,),
            in_specs=[
                pl.BlockSpec(
                    (groups, quarters, None, sides, None, rows, lanes),
                    lambda e, w: (0, 0, e, 0, w[0], 0, 0),
                ),
                pl.BlockSpec(
                    (quarters, None, sides, None, groups, rows, lanes), lambda e, w: (0, e, 0, w[1], 0, 0, 0)
                ),
            ],
            out_specs=pl.BlockSpec((1, 2, width, width), lambda e, w: (e, 0, 0, 0)),
        ),
        cost_estimate=pl.CostEstimate(
            flops=4 * groups * quarters * rows * width * width * mine,
            transcendentals=0,
            bytes_accessed=2 * read + mine * 2 * width * width * 4,
        ),
        name="cross",
    )(jnp.stack([half, jnp.int32(turn)]), own, other)


HOPS = [(1, 0, 0), (1, 1, 0), (1, 1, 1), (1, 1, 3), (1, 0, 1), (1, 0, 3), (1, 1, 2), (1, 0, 2)]
HOPS += [(0, 1, 0), (0, 0, 1), (0, 0, 3), (0, 1, 1), (0, 1, 3), (0, 0, 2), (0, 1, 2)]


def per_device(spectra, partner):
    windows, bins, _, parts, width = spectra.shape
    nl, ny = lax.axis_size("xl"), lax.axis_size("y")
    groups = nl * ny
    lanes, sides = LANES, width // LANES
    inner = lax.axis_size("z") * lax.axis_size("core")
    blocks = 2 * inner
    plane, xl, y = lax.axis_index("xh"), lax.axis_index("xl"), lax.axis_index("y")
    column = lax.axis_index(ZC)
    rounds = partner.shape[0]
    mine = bins // 2 // groups
    rows = windows // 4 * parts
    halves = (jnp.arange(blocks, dtype=jnp.int32)[None, :] > partner).astype(jnp.int32)

    joint = pack(spectra, groups).reshape(blocks * groups, 2, rows, lanes)
    holdings = lax.all_to_all(joint, ALL, split_axis=0, concat_axis=0, tiled=True)
    holdings = holdings.reshape(blocks, groups, 2, rows, lanes)

    def fetch(side):
        first = side * inner
        chosen = lax.dynamic_slice_in_dim(partner, first, inner, 1).T.reshape(-1)
        wanted = lax.dynamic_slice_in_dim(halves, first, inner, 1).T.reshape(-1)
        outgoing = pick(holdings, chosen, wanted).reshape(inner, rounds, groups, rows, lanes)
        incoming = lax.all_to_all(outgoing, ZC, split_axis=0, concat_axis=0, tiled=True)
        return incoming.reshape(2, mine, sides, rounds, groups, rows, lanes)

    away_other = fetch(1 - plane)
    kept_other = fetch(plane)

    by_plane = joint.reshape(2, inner, groups, 2, rows, lanes)
    own = [jnp.zeros((groups, inner, 2, rows, lanes), spectra.dtype) for _ in range(2)]

    def piece(fx, fl, dy):
        start = (plane ^ fx, 0, (xl ^ fl) * ny + (y + dy) % ny, 0, 0, 0)
        return lax.dynamic_slice(by_plane, start, (1, inner, 1, 2, rows, lanes)).reshape(1, inner, 2, rows, lanes)

    def put(part, fx, fl, dy):
        slot = (xl ^ fl) * ny + (y - dy) % ny
        own[fx] = lax.dynamic_update_slice(own[fx], part, (slot, 0, 0, 0, 0))

    put(piece(0, 0, 0), 0, 0, 0)
    for fx, fl, dy in HOPS:
        table = [
            ((cx * nl + cl) * ny + cy, ((cx ^ fx) * nl + (cl ^ fl)) * ny + (cy + dy) % ny)
            for cx in range(2)
            for cl in range(nl)
            for cy in range(ny)
        ]
        part = piece(fx, fl, dy)
        part = lax.ppermute(part, XY, table)
        put(part, fx, fl, dy)
    kept_own, away_own = (o.reshape(groups, 2, mine, sides, 2, rows, lanes) for o in own)

    scale = 1.0 / math.sqrt(windows * groups)
    backs = []
    for r in range(rounds):
        away = cross(away_own, away_other, halves[r][(1 - plane) * inner + column], r)
        backs.append(lax.ppermute(away, "xh", [(0, 1), (1, 0)]))
    results = []
    for r in range(rounds):
        kept = cross(kept_own, kept_other, halves[r][plane * inner + column], r)
        results.append((kept + backs[r]) * scale)
    return jnp.stack(results)[:, None]


def solution(mesh):
    fine = Mesh(mesh.devices.reshape(2, 4, 2, 2, 4), ALL)
    chan, tm = ("xh", "z", "core"), ("xl", "y")

    return jax.shard_map(
        per_device,
        mesh=fine,
        in_specs=(P(tm, None, chan, None, None), P()),
        out_specs=P(None, chan, tm, None, None, None),
        check_vma=False,
    )
```

```python
import functools
import math

import jax
import jax.numpy as jnp
from jax import lax
from jax.experimental import pallas as pl
from jax.experimental.pallas import tpu as pltpu
from jax.sharding import Mesh, PartitionSpec as P


ALL = ("xh", "z", "core", "xl", "y")
ZC = ("z", "core")
XY = ("xh", "xl", "y")
LANES = 128


def pack_kernel(groups, src, dst, buf, in_sem, out_sem):
    quarters, quarter, bins = buf.shape[:3]
    per = bins // 2 // groups

    def load(s):
        return pltpu.make_async_copy(src.at[pl.ds(s * quarter, quarter), :, 0], buf.at[s], in_sem.at[s])

    for s in range(quarters):
        load(s).start()
    for s in range(quarters):
        load(s).wait()
        for b in range(bins):
            h, rest = b // (bins // 2), b % (bins // 2)
            u, e = rest // per, rest % per
            for lh in range(buf.shape[-1] // LANES):
                pltpu.make_async_copy(
                    buf.at[s, :, b, :, pl.ds(lh * LANES, LANES)],
                    dst.at[s // 2, s % 2, e, lh, u, h],
                    out_sem.at[s],
                ).start()
    for s in range(quarters):
        pltpu.make_async_copy(src.at[pl.ds(s * quarter, quarter), :, 0], buf.at[s], out_sem.at[s]).wait()


def pack(spectra, groups):
    windows, bins, _, parts, width = spectra.shape
    quarter = windows // 4
    per, sides = bins // 2 // groups, width // LANES
    return pl.pallas_call(
        functools.partial(pack_kernel, groups),
        out_shape=jax.ShapeDtypeStruct((2, 2, per, sides, groups, 2, quarter, parts, LANES), spectra.dtype),
        in_specs=[pl.BlockSpec(memory_space=pl.ANY)],
        out_specs=pl.BlockSpec(memory_space=pl.ANY),
        scratch_shapes=[
            pltpu.VMEM((4, quarter, bins, parts, width), spectra.dtype),
            pltpu.SemaphoreType.DMA((4,)),
            pltpu.SemaphoreType.DMA((4,)),
        ],
        cost_estimate=pl.CostEstimate(flops=0, transcendentals=0, bytes_accessed=4 * spectra.size),
        name="pack",
    )(spectra)


def pick_kernel(blocks_ref, halves_ref, src, dst, buf, in_sem, out_sem):
    count = buf.shape[0]

    def load(i):
        return pltpu.make_async_copy(src.at[blocks_ref[i], :, halves_ref[i]], buf.at[i], in_sem.at[i])

    def store(i):
        return pltpu.make_async_copy(buf.at[i], dst.at[i], out_sem.at[i])

    for i in range(count):
        load(i).start()
    for i in range(count):
        load(i).wait()
        store(i).start()
    for i in range(count):
        store(i).wait()


def pick(holdings, chosen, halves):
    _, groups, _, rows, lanes = holdings.shape
    count = chosen.shape[0]
    shape = (count, groups, rows, lanes)
    return pl.pallas_call(
        pick_kernel,
        out_shape=jax.ShapeDtypeStruct(shape, holdings.dtype),
        grid_spec=pltpu.PrefetchScalarGridSpec(
            num_scalar_prefetch=2,
            grid=(),
            in_specs=[pl.BlockSpec(memory_space=pl.ANY)],
            out_specs=pl.BlockSpec(memory_space=pl.ANY),
            scratch_shapes=[
                pltpu.VMEM(shape, holdings.dtype),
                pltpu.SemaphoreType.DMA((count,)),
                pltpu.SemaphoreType.DMA((count,)),
            ],
        ),
        cost_estimate=pl.CostEstimate(flops=0, transcendentals=0, bytes_accessed=4 * math.prod(shape)),
        name="pick",
    )(chosen, halves, holdings)


def cross_kernel(fused, scale, slots_ref, wanted_ref, *refs):
    count = slots_ref.shape[0]
    pieces, other_ref = refs[:count], refs[count]
    out_ref, own_ref = refs[-2:]
    groups, quarters, sides, rows, lanes = own_ref.shape
    for k in range(count):
        own_ref[slots_ref[k]] = pieces[k][...]
    depth = groups * rows
    odd = lax.broadcasted_iota(jnp.int32, (depth // 8, 8, lanes * sides), 1) % 2 == 1
    real = None
    for q in range(quarters):
        a = jnp.concatenate([own_ref[:, q, s].reshape(depth, lanes) for s in range(sides)], axis=1)
        b = jnp.concatenate([other_ref[q, s].reshape(depth, lanes) for s in range(sides)], axis=1)
        tall = b.astype(jnp.float32).reshape(depth // 8, 8, lanes * sides)
        turned = jnp.where(odd, pltpu.roll(tall, 1, 1), -pltpu.roll(tall, 7, 1))
        turned = turned.reshape(depth, lanes * sides).astype(b.dtype)
        dims = (((0,), (0,)), ((), ()))
        re = lax.dot_general(a, b, dims, preferred_element_type=jnp.float32)
        im = lax.dot_general(a, turned, dims, preferred_element_type=jnp.float32)
        real, imag = (re, im) if real is None else (real + re, imag + im)
    if fused:
        back_ref = refs[count + 1]
        real, imag = (real + back_ref[0, 0]) * scale, (imag + back_ref[0, 1]) * scale
    out_ref[0, 0] = real
    out_ref[0, 1] = imag


def cross(pieces, slots, wanted, other, turn, back=None, scale=None, out=None):
    groups = len(pieces)
    quarters, mine, sides, _, rows, lanes = pieces[0].shape
    rounds = other.shape[3]
    width = sides * lanes
    read = groups * quarters * mine * sides * rows * lanes * 2
    piece = pl.BlockSpec((quarters, None, sides, None, rows, lanes), lambda e, n, w: (0, e, 0, w[turn], 0, 0))
    in_specs = [piece] * groups
    in_specs += [pl.BlockSpec((quarters, None, sides, None, groups, rows, lanes), lambda e, n, w: (0, e, 0, turn, 0, 0, 0))]
    one = pl.BlockSpec((1, 2, width, width), lambda e, n, w: (e, 0, 0, 0))
    operands = [slots, wanted, *pieces, other]
    out_spec, shape, aliases = one, (mine, 2, width, width), {}
    if back is not None:
        operands.append(back)
        in_specs.append(one)
        out_spec = pl.BlockSpec((None, None, 1, 2, width, width), lambda e, n, w: (turn, 0, e, 0, 0, 0))
        shape = (rounds, 1, mine, 2, width, width)
        if out is not None:
            aliases = {len(operands): 0}
            operands.append(out)
            in_specs.append(pl.BlockSpec(memory_space=pl.ANY))
    return pl.pallas_call(
        functools.partial(cross_kernel, back is not None, scale),
        out_shape=jax.ShapeDtypeStruct(shape, jnp.float32),
        grid_spec=pltpu.PrefetchScalarGridSpec(
            num_scalar_prefetch=2,
            grid=(mine,),
            in_specs=in_specs,
            out_specs=out_spec,
            scratch_shapes=[pltpu.VMEM((groups, quarters, sides, rows, lanes), pieces[0].dtype)],
        ),
        input_output_aliases=aliases,
        cost_estimate=pl.CostEstimate(
            flops=4 * groups * quarters * rows * width * width * mine,
            transcendentals=0,
            bytes_accessed=2 * read + mine * 2 * width * width * 4,
        ),
        name="cross",
    )(*operands)


def settle_kernel(scale, kept_ref, back_ref, before_ref, out_ref):
    out_ref[...] = (kept_ref[...] + back_ref[...]) * scale


def settle(kept, back, out, turn, scale):
    mine, _, width, _ = kept.shape
    one = pl.BlockSpec((1, 2, width, width), lambda e: (e, 0, 0, 0))
    return pl.pallas_call(
        functools.partial(settle_kernel, scale),
        out_shape=jax.ShapeDtypeStruct(out.shape, out.dtype),
        grid=(mine,),
        in_specs=[one, one, pl.BlockSpec(memory_space=pl.ANY)],
        out_specs=pl.BlockSpec((None, None, 1, 2, width, width), lambda e: (turn, 0, e, 0, 0, 0)),
        input_output_aliases={2: 0},
        cost_estimate=pl.CostEstimate(flops=2 * kept.size, transcendentals=0, bytes_accessed=12 * kept.size),
        name="settle",
    )(kept, back, out)


HOPS = [(1, 0, 0), (1, 1, 0), (1, 1, 1), (1, 1, 3), (1, 0, 1), (1, 0, 3), (1, 1, 2), (1, 0, 2)]
HOPS += [(0, 1, 0), (0, 0, 1), (0, 0, 3), (0, 1, 1), (0, 1, 3), (0, 0, 2), (0, 1, 2)]


def per_device(spectra, partner):
    windows, bins, _, parts, width = spectra.shape
    nl, ny = lax.axis_size("xl"), lax.axis_size("y")
    groups = nl * ny
    lanes, sides = LANES, width // LANES
    inner = lax.axis_size("z") * lax.axis_size("core")
    blocks = 2 * inner
    plane, xl, y = lax.axis_index("xh"), lax.axis_index("xl"), lax.axis_index("y")
    column = lax.axis_index(ZC)
    rounds = partner.shape[0]
    mine = bins // 2 // groups
    rows = windows // 4 * parts
    halves = (jnp.arange(blocks, dtype=jnp.int32)[None, :] > partner).astype(jnp.int32)

    joint = pack(spectra, groups).reshape(blocks * groups, 2, rows, lanes)
    holdings = lax.all_to_all(joint, ALL, split_axis=0, concat_axis=0, tiled=True)
    holdings = holdings.reshape(blocks, groups, 2, rows, lanes)

    def fetch(side):
        first = side * inner
        chosen = lax.dynamic_slice_in_dim(partner, first, inner, 1).T.reshape(-1)
        wanted = lax.dynamic_slice_in_dim(halves, first, inner, 1).T.reshape(-1)
        outgoing = pick(holdings, chosen, wanted).reshape(inner, rounds, groups, rows, lanes)
        incoming = lax.all_to_all(outgoing, ZC, split_axis=0, concat_axis=0, tiled=True)
        return incoming.reshape(2, mine, sides, rounds, groups, rows, lanes)

    away_other = fetch(1 - plane)
    kept_other = fetch(plane)

    by_plane = joint.reshape(2, inner, groups, 2, rows, lanes)
    shape = (2, mine, sides, 2, rows, lanes)

    def piece(fx, fl, dy):
        start = (plane ^ fx, 0, (xl ^ fl) * ny + (y + dy) % ny, 0, 0, 0)
        part = lax.dynamic_slice(by_plane, start, (1, inner, 1, 2, rows, lanes))
        return part.reshape(inner, 2, rows, lanes)

    own = [[piece(0, 0, 0).reshape(shape)], []]
    for fx, fl, dy in HOPS:
        table = [
            ((cx * nl + cl) * ny + cy, ((cx ^ fx) * nl + (cl ^ fl)) * ny + (cy + dy) % ny)
            for cx in range(2)
            for cl in range(nl)
            for cy in range(ny)
        ]
        part = piece(fx, fl, dy)
        part = lax.ppermute(part, XY, table)
        own[fx].append(part.reshape(shape))
    places = [jnp.array([fl * ny for g, fl, _ in order if g == fx]) for fx, order in ((0, [(0, 0, 0)] + HOPS), (1, HOPS))]
    steps = [jnp.array([dy for g, _, dy in order if g == fx]) for fx, order in ((0, [(0, 0, 0)] + HOPS), (1, HOPS))]
    slots = [((xl * ny) ^ p) + (y - s) % ny for p, s in zip(places, steps)]
    wanted = [lax.dynamic_index_in_dim(halves, (plane ^ fx) * inner + column, 1, keepdims=False) for fx in range(2)]

    scale = 1.0 / math.sqrt(windows * groups)
    backs = []
    for r in range(rounds):
        away = cross(own[1], slots[1], wanted[1], away_other, r)
        backs.append(lax.ppermute(away, "xh", [(0, 1), (1, 0)]))
    last = cross(own[0], slots[0], wanted[0], kept_other, rounds - 1)
    out = None
    for r in range(rounds - 1):
        out = cross(own[0], slots[0], wanted[0], kept_other, r, backs[r], scale, out)
    return settle(last, backs[-1], out, rounds - 1, scale)


def solution(mesh):
    fine = Mesh(mesh.devices.reshape(2, 4, 2, 2, 4), ALL)
    chan, tm = ("xh", "z", "core"), ("xl", "y")

    return jax.shard_map(
        per_device,
        mesh=fine,
        in_specs=(P(tm, None, chan, None, None), P()),
        out_specs=P(None, chan, tm, None, None, None),
        check_vma=False,
    )
```

```python
import functools
import math

import jax
import jax.numpy as jnp
from jax import lax
from jax.experimental import pallas as pl
from jax.experimental.pallas import tpu as pltpu
from jax.sharding import Mesh, PartitionSpec as P


ALL = ("xh", "z", "core", "xl", "y")
ZC = ("z", "core")
XY = ("xh", "xl", "y")
LANES = 128


def pack_kernel(groups, src, dst, buf, in_sem, out_sem):
    quarters, quarter, bins = buf.shape[:3]
    per = bins // 2 // groups

    def load(s):
        return pltpu.make_async_copy(src.at[pl.ds(s * quarter, quarter), :, 0], buf.at[s], in_sem.at[s])

    for s in range(quarters):
        load(s).start()
    for s in range(quarters):
        load(s).wait()
        for b in range(bins):
            h, rest = b // (bins // 2), b % (bins // 2)
            u, e = rest // per, rest % per
            for lh in range(buf.shape[-1] // LANES):
                pltpu.make_async_copy(
                    buf.at[s, :, b, :, pl.ds(lh * LANES, LANES)],
                    dst.at[s // 2, s % 2, e, lh, u, h],
                    out_sem.at[s],
                ).start()
    for s in range(quarters):
        pltpu.make_async_copy(src.at[pl.ds(s * quarter, quarter), :, 0], buf.at[s], out_sem.at[s]).wait()


def pack(spectra, groups):
    windows, bins, _, parts, width = spectra.shape
    quarter = windows // 4
    per, sides = bins // 2 // groups, width // LANES
    return pl.pallas_call(
        functools.partial(pack_kernel, groups),
        out_shape=jax.ShapeDtypeStruct((2, 2, per, sides, groups, 2, quarter, parts, LANES), spectra.dtype),
        in_specs=[pl.BlockSpec(memory_space=pl.ANY)],
        out_specs=pl.BlockSpec(memory_space=pl.ANY),
        scratch_shapes=[
            pltpu.VMEM((4, quarter, bins, parts, width), spectra.dtype),
            pltpu.SemaphoreType.DMA((4,)),
            pltpu.SemaphoreType.DMA((4,)),
        ],
        cost_estimate=pl.CostEstimate(flops=0, transcendentals=0, bytes_accessed=4 * spectra.size),
        name="pack",
    )(spectra)


def pick_kernel(entries, meta, src, *refs):
    outs, (buf, in_sem, out_sem) = refs[:-3], refs[-3:]
    targets, groups = buf.shape[0], src.shape[1]
    if len(outs) == 1:
        outs = [outs[0].at[k] for k in range(targets)]
    steps = (buf.shape[1] - entries * groups) // 2

    def loads(k):
        copies = []
        for i in range(entries):
            n = k * entries + i
            copies.append((src.at[meta[n], :, meta[targets * entries + n]], buf.at[k, pl.ds(i * groups, groups)]))
        for i in range(steps):
            block, group = meta[2 * targets * entries + k], meta[2 * targets * entries + targets + i]
            copies.append((src.at[block, group], buf.at[k, pl.ds(entries * groups + 2 * i, 2)]))
        return [pltpu.make_async_copy(x, y, in_sem.at[k, i]) for i, (x, y) in enumerate(copies)]

    for k in range(targets):
        for copy in loads(k):
            copy.start()
    for k in range(targets):
        for copy in loads(k):
            copy.wait()
        pltpu.make_async_copy(buf.at[k], outs[k], out_sem.at[k]).start()
    for k in range(targets):
        pltpu.make_async_copy(buf.at[k], outs[k], out_sem.at[k]).wait()


def pick(holdings, blocks, halves, own_blocks, own_groups, joined):
    _, groups, _, rows, lanes = holdings.shape
    targets, entries = blocks.shape
    steps = own_groups.shape[0]
    units = entries * groups + 2 * steps
    meta = jnp.concatenate([blocks.reshape(-1), halves.reshape(-1), own_blocks, own_groups])
    whole = pl.BlockSpec(memory_space=pl.ANY)
    shapes = [(targets, units, rows, lanes)] if joined else [(units, rows, lanes)] * targets
    return pl.pallas_call(
        functools.partial(pick_kernel, entries),
        out_shape=[jax.ShapeDtypeStruct(shape, holdings.dtype) for shape in shapes],
        grid_spec=pltpu.PrefetchScalarGridSpec(
            num_scalar_prefetch=1,
            grid=(),
            in_specs=[whole],
            out_specs=[whole] * len(shapes),
            scratch_shapes=[
                pltpu.VMEM((targets, units, rows, lanes), holdings.dtype),
                pltpu.SemaphoreType.DMA((targets, entries + steps)),
                pltpu.SemaphoreType.DMA((targets,)),
            ],
        ),
        cost_estimate=pl.CostEstimate(flops=0, transcendentals=0, bytes_accessed=4 * targets * units * rows * lanes),
        name="pick",
    )(meta, holdings)


def cross_kernel(counts, mine, fused, scale, wanted_ref, places_ref, *refs):
    whole, steps, shares = counts
    pieces, refs = refs[:whole], refs[whole:]
    single, refs = refs[: shares * steps], refs[shares * steps :]
    others, refs = refs[:shares], refs[shares:]
    out_ref, own_ref, other_ref = refs[-3:]
    _, groups, rows, lanes = own_ref.shape
    for k in range(whole):
        own_ref[:, places_ref[shares + k]] = pieces[k][...]
    for k in range(shares):
        other_ref[places_ref[k]] = others[k][...]
        for i in range(steps):
            own_ref[k, places_ref[shares + whole + i]] = single[k * steps + i][...]
    sides = 2
    quarters = shares // (mine * sides)
    depth = groups * rows
    odd = lax.broadcasted_iota(jnp.int32, (depth // 8, 8, lanes * sides), 1) % 2 == 1
    for e in range(mine):
        real = None
        for q in range(quarters):
            at = (q * mine + e) * sides
            a = jnp.concatenate([own_ref[at + s].reshape(depth, lanes) for s in range(sides)], axis=1)
            b = jnp.concatenate([other_ref[at + s].reshape(depth, lanes) for s in range(sides)], axis=1)
            tall = b.astype(jnp.float32).reshape(depth // 8, 8, lanes * sides)
            turned = jnp.where(odd, pltpu.roll(tall, 1, 1), -pltpu.roll(tall, 7, 1))
            turned = turned.reshape(depth, lanes * sides).astype(b.dtype)
            dims = (((0,), (0,)), ((), ()))
            re = lax.dot_general(a, b, dims, preferred_element_type=jnp.float32)
            im = lax.dot_general(a, turned, dims, preferred_element_type=jnp.float32)
            real, imag = (re, im) if real is None else (real + re, imag + im)
        if fused:
            back_ref = refs[0]
            real, imag = (real + back_ref[e, 0]) * scale, (imag + back_ref[e, 1]) * scale
        out_ref[e, 0] = real
        out_ref[e, 1] = imag


def cross(pieces, single, others, entry, first, places, wanted, mine, turn, rounds, back=None, scale=None, out=None):
    shares, _, rows, lanes = pieces[0].shape
    width = 2 * lanes
    steps = 0 if single is None else places.shape[0] - shares - len(pieces)
    groups = len(pieces) + steps
    in_specs = [pl.BlockSpec((shares, None, rows, lanes), lambda i, w, p: (0, w[turn], 0, 0))] * len(pieces)
    operands = [wanted, places, *pieces]
    for k in range(shares):
        for i in range(steps):
            operands.append(single)
            in_specs.append(
                pl.BlockSpec((None, None, rows, lanes), lambda n, w, p, k=k, at=first + 2 * i: (k, at + w[turn], 0, 0))
            )
    if isinstance(others, list):
        operands += others
        in_specs += [pl.BlockSpec((groups, rows, lanes), lambda i, w, p: (entry, 0, 0))] * shares
    else:
        operands += [others] * shares
        in_specs += [
            pl.BlockSpec((None, groups, rows, lanes), lambda i, w, p, k=k: (k, entry, 0, 0)) for k in range(shares)
        ]
    one = pl.BlockSpec((mine, 2, width, width), lambda i, w, p: (0, 0, 0, 0))
    out_spec, shape, aliases = one, (mine, 2, width, width), {}
    if back is not None:
        operands.append(back)
        in_specs.append(one)
        out_spec = pl.BlockSpec((None, None, mine, 2, width, width), lambda i, w, p: (turn, 0, 0, 0, 0, 0))
        shape = (rounds, 1, mine, 2, width, width)
        if out is not None:
            aliases = {len(operands): 0}
            operands.append(out)
            in_specs.append(pl.BlockSpec(memory_space=pl.ANY))
    return pl.pallas_call(
        functools.partial(cross_kernel, (len(pieces), steps, shares), mine, back is not None, scale),
        out_shape=jax.ShapeDtypeStruct(shape, jnp.float32),
        grid_spec=pltpu.PrefetchScalarGridSpec(
            num_scalar_prefetch=2,
            grid=(1,),
            in_specs=in_specs,
            out_specs=out_spec,
            scratch_shapes=[pltpu.VMEM((shares, groups, rows, lanes), pieces[0].dtype)] * 2,
        ),
        input_output_aliases=aliases,
        cost_estimate=pl.CostEstimate(
            flops=2 * shares * groups * rows * width * width,
            transcendentals=0,
            bytes_accessed=4 * shares * groups * rows * lanes + mine * 2 * width * width * 4,
        ),
        name="cross",
    )(*operands)


HOPS = [(1, 1, 0), (0, 1, 0), (1, 1, 1), (1, 0, 0), (0, 1, 1), (1, 1, 3), (1, 0, 3), (0, 1, 3), (1, 1, 2), (0, 1, 2)]
HOPS += [(0, 0, 1), (0, 0, 3), (0, 0, 2)]
FETCHED = (1, 2)
TURNS = [(0, 0), (1, 0), (3, 0), (1, 1), (3, 1), (2, 0), (2, 1), (0, 1)]
PARTS = [[(0, 0), (0, 1)], [(0, 2), (1, 0)], [(1, 1), (1, 2)]]


def per_device(spectra, partner):
    windows, bins, _, parts, _ = spectra.shape
    nl, ny = lax.axis_size("xl"), lax.axis_size("y")
    nz, nc = lax.axis_size("z"), lax.axis_size("core")
    groups, inner = nl * ny, nz * nc
    lanes = LANES
    blocks = 2 * inner
    plane, xl, y = lax.axis_index("xh"), lax.axis_index("xl"), lax.axis_index("y")
    z, core = lax.axis_index("z"), lax.axis_index("core")
    rounds = partner.shape[0]
    mine = bins // 2 // groups
    rows = windows // 4 * parts

    joint = pack(spectra, groups).reshape(blocks * groups, 2, rows, lanes)
    holdings = lax.all_to_all(joint, ALL, split_axis=0, concat_axis=0, tiled=True)
    holdings = holdings.reshape(blocks, groups, 2, rows, lanes)

    dz, dc = jnp.array([t[0] for t in TURNS]), jnp.array([t[1] for t in TURNS])
    every = jnp.arange(inner, dtype=jnp.int32)
    turned = ((z + dz) % nz) * nc + (core + dc) % nc
    shares = ((z - dz) % nz) * nc + (core - dc) % nc
    planes = jnp.stack([1 - plane, plane])
    seat = planes[:, None] * inner + jnp.concatenate([every, turned])[None, :]
    mates = partner[:, seat]
    sides = (seat[None] > mates).astype(jnp.int32)
    fetched_groups = xl * ny + (y - jnp.array(FETCHED)) % ny

    def fetch(part):
        entries, joined = PARTS[part], part == 0
        at = slice(0, inner) if joined else slice(inner, None)
        chosen = jnp.stack([mates[r, side, at] for side, r in entries], axis=1)
        wanted = jnp.stack([sides[r, side, at] for side, r in entries], axis=1)
        extra = fetched_groups if joined else fetched_groups[:0]
        outs = pick(holdings, chosen, wanted, seat[0, at], extra, joined)
        if joined:
            return lax.all_to_all(outs[0], ZC, split_axis=0, concat_axis=0, tiled=True)
        arrived = [outs[0]]
        for k, (a, b) in enumerate(TURNS[1:]):
            table = [
                (cz * nc + cc, ((cz + a) % nz) * nc + (cc + b) % nc) for cz in range(nz) for cc in range(nc)
            ]
            arrived.append(lax.ppermute(outs[k + 1], ZC, table))
        return arrived

    others = [fetch(part) for part in range(len(PARTS))]

    by_plane = joint.reshape(2, inner, groups, 2, rows, lanes)

    def piece(fx, fl, dy):
        start = (plane ^ fx, 0, (xl ^ fl) * ny + (y + dy) % ny, 0, 0, 0)
        part = lax.dynamic_slice(by_plane, start, (1, inner, 1, 2, rows, lanes))
        return part.reshape(inner, 2, rows, lanes)

    own = [[piece(0, 0, 0)], []]
    for fx, fl, dy in HOPS:
        table = [
            ((cx * nl + cl) * ny + cy, ((cx ^ fx) * nl + (cl ^ fl)) * ny + (cy + dy) % ny)
            for cx in range(2)
            for cl in range(nl)
            for cy in range(ny)
        ]
        part = piece(fx, fl, dy)
        own[fx].append(lax.ppermute(part, XY, table))

    def places(order):
        flips, steps = jnp.array([fl for fl, _ in order]), jnp.array([dy for _, dy in order])
        slots = (xl ^ flips) * ny + (y - steps) % ny
        return [jnp.concatenate([every, slots]), jnp.concatenate([shares, slots])]

    away_places = places([(fl, dy) for fx, fl, dy in HOPS if fx == 1] + [(0, dy) for dy in FETCHED])
    kept_places = places([(0, 0)] + [(fl, dy) for fx, fl, dy in HOPS if fx == 0])
    wanted = (planes[:, None, None] * inner + z * nc + core)[:, :, 0]
    mine_half = [(wanted[i, 0] > lax.dynamic_index_in_dim(partner, wanted[i, 0], 1, False)).astype(jnp.int32) for i in range(2)]

    where = {pair: (p, i) for p, pairs in enumerate(PARTS) for i, pair in enumerate(pairs)}
    first = len(PARTS[0]) * groups
    scale = 1.0 / math.sqrt(windows * groups)
    backs = []
    for r in range(rounds):
        p, i = where[0, r]
        away = cross(own[1], others[0], others[p], i, first, away_places[p > 0], mine_half[0], mine, r, rounds)
        backs.append(lax.ppermute(away, "xh", [(0, 1), (1, 0)]))
    out = None
    for r in range(rounds):
        p, i = where[1, r]
        out = cross(own[0], None, others[p], i, 0, kept_places[p > 0], mine_half[1], mine, r, rounds, backs[r], scale, out)
    return out


def solution(mesh):
    fine = Mesh(mesh.devices.reshape(2, 4, 2, 2, 4), ALL)
    chan, tm = ("xh", "z", "core"), ("xl", "y")

    return jax.shard_map(
        per_device,
        mesh=fine,
        in_specs=(P(tm, None, chan, None, None), P()),
        out_specs=P(None, chan, tm, None, None, None),
        check_vma=False,
    )
```

```python
import functools
import math

import jax
import jax.numpy as jnp
from jax import lax
from jax.experimental import pallas as pl
from jax.experimental.pallas import tpu as pltpu
from jax.sharding import Mesh, PartitionSpec as P


ALL = ("xh", "z", "core", "xl", "y")
ZC = ("z", "core")
XY = ("xh", "xl", "y")
LANES = 128


def pack_kernel(groups, src, dst, buf, in_sem, out_sem):
    quarters, quarter, bins = buf.shape[:3]
    per = bins // 2 // groups

    def load(s):
        return pltpu.make_async_copy(src.at[pl.ds(s * quarter, quarter), :, 0], buf.at[s], in_sem.at[s])

    for s in range(quarters):
        load(s).start()
    for s in range(quarters):
        load(s).wait()
        for b in range(bins):
            h, rest = b // (bins // 2), b % (bins // 2)
            u, e = rest // per, rest % per
            for lh in range(buf.shape[-1] // LANES):
                pltpu.make_async_copy(
                    buf.at[s, :, b, :, pl.ds(lh * LANES, LANES)],
                    dst.at[s // 2, s % 2, e, lh, u, h],
                    out_sem.at[s],
                ).start()
    for s in range(quarters):
        pltpu.make_async_copy(src.at[pl.ds(s * quarter, quarter), :, 0], buf.at[s], out_sem.at[s]).wait()


def pack(spectra, groups):
    windows, bins, _, parts, width = spectra.shape
    quarter = windows // 4
    per, sides = bins // 2 // groups, width // LANES
    return pl.pallas_call(
        functools.partial(pack_kernel, groups),
        out_shape=jax.ShapeDtypeStruct((2, 2, per, sides, groups, 2, quarter, parts, LANES), spectra.dtype),
        in_specs=[pl.BlockSpec(memory_space=pl.ANY)],
        out_specs=pl.BlockSpec(memory_space=pl.ANY),
        scratch_shapes=[
            pltpu.VMEM((4, quarter, bins, parts, width), spectra.dtype),
            pltpu.SemaphoreType.DMA((4,)),
            pltpu.SemaphoreType.DMA((4,)),
        ],
        cost_estimate=pl.CostEstimate(flops=0, transcendentals=0, bytes_accessed=4 * spectra.size),
        name="pack",
    )(spectra)


def pick_kernel(entries, meta, src, *refs):
    outs, (buf, in_sem, out_sem) = refs[:-3], refs[-3:]
    targets, groups = buf.shape[0], src.shape[1]
    if len(outs) == 1:
        outs = [outs[0].at[k] for k in range(targets)]
    steps = (buf.shape[1] - entries * groups) // 2

    def loads(k):
        copies = []
        for i in range(entries):
            n = k * entries + i
            copies.append((src.at[meta[n], :, meta[targets * entries + n]], buf.at[k, pl.ds(i * groups, groups)]))
        for i in range(steps):
            block, group = meta[2 * targets * entries + k], meta[2 * targets * entries + targets + i]
            copies.append((src.at[block, group], buf.at[k, pl.ds(entries * groups + 2 * i, 2)]))
        return [pltpu.make_async_copy(x, y, in_sem.at[k, i]) for i, (x, y) in enumerate(copies)]

    for k in range(targets):
        for copy in loads(k):
            copy.start()
    for k in range(targets):
        for copy in loads(k):
            copy.wait()
        pltpu.make_async_copy(buf.at[k], outs[k], out_sem.at[k]).start()
    for k in range(targets):
        pltpu.make_async_copy(buf.at[k], outs[k], out_sem.at[k]).wait()


def pick(holdings, blocks, halves, own_blocks, own_groups, joined):
    _, groups, _, rows, lanes = holdings.shape
    targets, entries = blocks.shape
    steps = own_groups.shape[0]
    units = entries * groups + 2 * steps
    meta = jnp.concatenate([blocks.reshape(-1), halves.reshape(-1), own_blocks, own_groups])
    whole = pl.BlockSpec(memory_space=pl.ANY)
    shapes = [(targets, units, rows, lanes)] if joined else [(units, rows, lanes)] * targets
    return pl.pallas_call(
        functools.partial(pick_kernel, entries),
        out_shape=[jax.ShapeDtypeStruct(shape, holdings.dtype) for shape in shapes],
        grid_spec=pltpu.PrefetchScalarGridSpec(
            num_scalar_prefetch=1,
            grid=(),
            in_specs=[whole],
            out_specs=[whole] * len(shapes),
            scratch_shapes=[
                pltpu.VMEM((targets, units, rows, lanes), holdings.dtype),
                pltpu.SemaphoreType.DMA((targets, entries + steps)),
                pltpu.SemaphoreType.DMA((targets,)),
            ],
        ),
        cost_estimate=pl.CostEstimate(flops=0, transcendentals=0, bytes_accessed=4 * targets * units * rows * lanes),
        name="pick",
    )(meta, holdings)


def cross_kernel(counts, mine, fused, scale, wanted_ref, places_ref, *refs):
    whole, steps, shares = counts
    pieces, refs = refs[:whole], refs[whole:]
    single, refs = refs[: shares * steps], refs[shares * steps :]
    others, refs = refs[:shares], refs[shares:]
    out_ref, own_ref, other_ref = refs[-3:]
    _, groups, rows, lanes = own_ref.shape
    for k in range(whole):
        own_ref[:, places_ref[shares + k]] = pieces[k][...]
    for k in range(shares):
        other_ref[places_ref[k]] = others[k][...]
        for i in range(steps):
            own_ref[k, places_ref[shares + whole + i]] = single[k * steps + i][...]
    sides = 2
    quarters = shares // (mine * sides)
    depth = groups * rows
    odd = lax.broadcasted_iota(jnp.int32, (quarters * depth // 8, 8, lanes * sides), 1) % 2 == 1
    for e in range(mine):
        at = [[(q * mine + e) * sides + s for q in range(quarters)] for s in range(sides)]
        a = jnp.concatenate(
            [jnp.concatenate([own_ref[n].reshape(depth, lanes) for n in rest], axis=0) for rest in at], axis=1
        )
        b = jnp.concatenate(
            [jnp.concatenate([other_ref[n].reshape(depth, lanes) for n in rest], axis=0) for rest in at], axis=1
        )
        tall = b.astype(jnp.float32).reshape(quarters * depth // 8, 8, lanes * sides)
        turned = jnp.where(odd, pltpu.roll(tall, 1, 1), -pltpu.roll(tall, 7, 1))
        turned = turned.reshape(quarters * depth, lanes * sides).astype(b.dtype)
        both = jnp.concatenate([b, turned], axis=1)
        both = lax.dot_general(a, both, (((0,), (0,)), ((), ())), preferred_element_type=jnp.float32)
        real, imag = both[:, : lanes * sides], both[:, lanes * sides :]
        if fused:
            back_ref = refs[0]
            real, imag = (real + back_ref[e, 0]) * scale, (imag + back_ref[e, 1]) * scale
        out_ref[e, 0] = real
        out_ref[e, 1] = imag


def cross(pieces, single, others, entry, first, places, wanted, mine, turn, rounds, back=None, scale=None, out=None):
    shares, _, rows, lanes = pieces[0].shape
    width = 2 * lanes
    steps = 0 if single is None else places.shape[0] - shares - len(pieces)
    groups = len(pieces) + steps
    in_specs = [pl.BlockSpec((shares, None, rows, lanes), lambda i, w, p: (0, w[turn], 0, 0))] * len(pieces)
    operands = [wanted, places, *pieces]
    for k in range(shares):
        for i in range(steps):
            operands.append(single)
            in_specs.append(
                pl.BlockSpec((None, None, rows, lanes), lambda n, w, p, k=k, at=first + 2 * i: (k, at + w[turn], 0, 0))
            )
    if isinstance(others, list):
        operands += others
        in_specs += [pl.BlockSpec((groups, rows, lanes), lambda i, w, p: (entry, 0, 0))] * shares
    else:
        operands += [others] * shares
        in_specs += [
            pl.BlockSpec((None, groups, rows, lanes), lambda i, w, p, k=k: (k, entry, 0, 0)) for k in range(shares)
        ]
    one = pl.BlockSpec((mine, 2, width, width), lambda i, w, p: (0, 0, 0, 0))
    out_spec, shape, aliases = one, (mine, 2, width, width), {}
    if back is not None:
        operands.append(back)
        in_specs.append(one)
        out_spec = pl.BlockSpec((None, None, mine, 2, width, width), lambda i, w, p: (turn, 0, 0, 0, 0, 0))
        shape = (rounds, 1, mine, 2, width, width)
        if out is not None:
            aliases = {len(operands): 0}
            operands.append(out)
            in_specs.append(pl.BlockSpec(memory_space=pl.ANY))
    return pl.pallas_call(
        functools.partial(cross_kernel, (len(pieces), steps, shares), mine, back is not None, scale),
        out_shape=jax.ShapeDtypeStruct(shape, jnp.float32),
        grid_spec=pltpu.PrefetchScalarGridSpec(
            num_scalar_prefetch=2,
            grid=(1,),
            in_specs=in_specs,
            out_specs=out_spec,
            scratch_shapes=[pltpu.VMEM((shares, groups, rows, lanes), pieces[0].dtype)] * 2,
        ),
        input_output_aliases=aliases,
        cost_estimate=pl.CostEstimate(
            flops=2 * shares * groups * rows * width * width,
            transcendentals=0,
            bytes_accessed=4 * shares * groups * rows * lanes + mine * 2 * width * width * 4,
        ),
        name="cross",
    )(*operands)


HOPS = [(1, 1, 0), (0, 1, 0), (1, 1, 1), (1, 0, 0), (0, 1, 1), (1, 1, 3), (1, 0, 3), (0, 1, 3), (1, 1, 2), (0, 1, 2)]
HOPS += [(0, 0, 1), (0, 0, 3), (0, 0, 2)]
FETCHED = (1, 2)
TURNS = [(0, 0), (1, 0), (3, 0), (1, 1), (3, 1), (2, 0), (2, 1), (0, 1)]
PARTS = [[(0, 0)], [(0, 1), (0, 2)], [(1, 0), (1, 1)], [(1, 2)]]


def per_device(spectra, partner):
    windows, bins, _, parts, _ = spectra.shape
    nl, ny = lax.axis_size("xl"), lax.axis_size("y")
    nz, nc = lax.axis_size("z"), lax.axis_size("core")
    groups, inner = nl * ny, nz * nc
    lanes = LANES
    blocks = 2 * inner
    plane, xl, y = lax.axis_index("xh"), lax.axis_index("xl"), lax.axis_index("y")
    z, core = lax.axis_index("z"), lax.axis_index("core")
    rounds = partner.shape[0]
    mine = bins // 2 // groups
    rows = windows // 4 * parts

    joint = pack(spectra, groups).reshape(blocks * groups, 2, rows, lanes)
    holdings = lax.all_to_all(joint, ALL, split_axis=0, concat_axis=0, tiled=True)
    holdings = holdings.reshape(blocks, groups, 2, rows, lanes)

    dz, dc = jnp.array([t[0] for t in TURNS]), jnp.array([t[1] for t in TURNS])
    every = jnp.arange(inner, dtype=jnp.int32)
    turned = ((z + dz) % nz) * nc + (core + dc) % nc
    shares = ((z - dz) % nz) * nc + (core - dc) % nc
    planes = jnp.stack([1 - plane, plane])
    seat = planes[:, None] * inner + jnp.concatenate([every, turned])[None, :]
    mates = partner[:, seat]
    sides = (seat[None] > mates).astype(jnp.int32)
    fetched_groups = xl * ny + (y - jnp.array(FETCHED)) % ny

    def fetch(part):
        entries, joined = PARTS[part], part == 0
        at = slice(0, inner) if joined else slice(inner, None)
        chosen = jnp.stack([mates[r, side, at] for side, r in entries], axis=1)
        wanted = jnp.stack([sides[r, side, at] for side, r in entries], axis=1)
        extra = fetched_groups if joined else fetched_groups[:0]
        outs = pick(holdings, chosen, wanted, seat[0, at], extra, joined)
        if joined:
            return lax.all_to_all(outs[0], ZC, split_axis=0, concat_axis=0, tiled=True)
        arrived = [outs[0]]
        for k, (a, b) in enumerate(TURNS[1:]):
            table = [
                (cz * nc + cc, ((cz + a) % nz) * nc + (cc + b) % nc) for cz in range(nz) for cc in range(nc)
            ]
            arrived.append(lax.ppermute(outs[k + 1], ZC, table))
        return arrived

    others = [fetch(part) for part in range(len(PARTS))]

    by_plane = joint.reshape(2, inner, groups, 2, rows, lanes)

    def piece(fx, fl, dy):
        start = (plane ^ fx, 0, (xl ^ fl) * ny + (y + dy) % ny, 0, 0, 0)
        part = lax.dynamic_slice(by_plane, start, (1, inner, 1, 2, rows, lanes))
        return part.reshape(inner, 2, rows, lanes)

    own = [[piece(0, 0, 0)], []]
    for fx, fl, dy in HOPS:
        table = [
            ((cx * nl + cl) * ny + cy, ((cx ^ fx) * nl + (cl ^ fl)) * ny + (cy + dy) % ny)
            for cx in range(2)
            for cl in range(nl)
            for cy in range(ny)
        ]
        part = piece(fx, fl, dy)
        own[fx].append(lax.ppermute(part, XY, table))

    def places(order):
        flips, steps = jnp.array([fl for fl, _ in order]), jnp.array([dy for _, dy in order])
        slots = (xl ^ flips) * ny + (y - steps) % ny
        return [jnp.concatenate([every, slots]), jnp.concatenate([shares, slots])]

    away_places = places([(fl, dy) for fx, fl, dy in HOPS if fx == 1] + [(0, dy) for dy in FETCHED])
    kept_places = places([(0, 0)] + [(fl, dy) for fx, fl, dy in HOPS if fx == 0])
    wanted = (planes[:, None, None] * inner + z * nc + core)[:, :, 0]
    mine_half = [(wanted[i, 0] > lax.dynamic_index_in_dim(partner, wanted[i, 0], 1, False)).astype(jnp.int32) for i in range(2)]

    where = {pair: (p, i) for p, pairs in enumerate(PARTS) for i, pair in enumerate(pairs)}
    first = len(PARTS[0]) * groups
    scale = 1.0 / math.sqrt(windows * groups)
    backs = []
    for r in range(rounds):
        p, i = where[0, r]
        away = cross(own[1], others[0], others[p], i, first, away_places[p > 0], mine_half[0], mine, r, rounds)
        backs.append(lax.ppermute(away, "xh", [(0, 1), (1, 0)]))
    out = None
    for r in range(rounds):
        p, i = where[1, r]
        out = cross(own[0], None, others[p], i, 0, kept_places[p > 0], mine_half[1], mine, r, rounds, backs[r], scale, out)
    return out


def solution(mesh):
    fine = Mesh(mesh.devices.reshape(2, 4, 2, 2, 4), ALL)
    chan, tm = ("xh", "z", "core"), ("xl", "y")

    return jax.shard_map(
        per_device,
        mesh=fine,
        in_specs=(P(tm, None, chan, None, None), P()),
        out_specs=P(None, chan, tm, None, None, None),
        check_vma=False,
    )
```
